32 devices in a mesh: shard: 4 (over x, core), ctx: 4 (over z), tp: 2 (over y).
Axes of the slice: x: 2, y: 2, z: 4, core: 2. Of those that a mesh axis runs over, the one named last changes fastest.
Arguments:
- hidden_in: bfloat16 [4096, 2048], P(('shard', 'ctx')), may hold values from -6 to 6
- gain_attn: bfloat16 [2048], P(('shard', 'ctx')), may hold values from 0.5 to 1.5
- w_qkv: bfloat16 [3, 2048, 2048], P(None, ('shard', 'ctx'), 'tp'), may hold values from -1 to 1
- w_out: bfloat16 [2048, 2048], P('tp', ('shard', 'ctx')), may hold values from -0.5 to 0.5
- gain_mlp: bfloat16 [2048], P(('shard', 'ctx')), may hold values from 0.5 to 1.5
- w_gate_up: bfloat16 [2, 2048, 8192], P(None, ('shard', 'ctx'), 'tp'), may hold values from -0.125 to 0.125
- w_down: bfloat16 [8192, 2048], P('tp', ('shard', 'ctx')), may hold values from -0.0625 to 0.0625
- segments: int32 [4, 1024], P('shard'), may hold values from 0 to 3, never falling along the last dimension, each value on 1 to 512 neighbouring positions
- cotangent: bfloat16 [4096, 2048], P(('shard', 'ctx')), may hold values from -6 to 6
Outputs:
- block_out: bfloat16 [4096, 2048], P(('shard', 'ctx'))
- grad_input: float32 [4096, 2048], P(('shard', 'ctx'))
- grad_gain_attn: float32 [2048], P(('shard', 'ctx'))
- grad_w_qkv: float32 [3, 2048, 2048], P(None, ('shard', 'ctx'), 'tp')
- grad_w_out: float32 [2048, 2048], P('tp', ('shard', 'ctx'))
- grad_gain_mlp: float32 [2048], P(('shard', 'ctx'))
- grad_w_gate_up: float32 [2, 2048, 8192], P(None, ('shard', 'ctx'), 'tp')
- grad_w_down: float32 [8192, 2048], P('tp', ('shard', 'ctx'))
The draws below stay inside these ranges and needn't reach their ends.
Inputs may be any that keep to these rules, and one draw needn't show every extreme that they name: `segments`: each row holds one group's 1024 segment numbers; they never fall, and each segment covers 1 to 512 positions, one exactly 512.
All inputs are finite; a program needn't handle non-finite values.
Results may differ from the reference program's by a relative error of at most 0.025.
Values may be sent and summed in bfloat16 or wider, within the bound.
No kernel may reach another device: no remote copies, remote signals or barrier semaphores. Data moves between devices by JAX's collectives and lax.ppermute only.
A program may use at most 256 MiB of HBM per device.

```python
import math
import jax
import jax.numpy as jnp
import numpy as np
from jax import lax

D = 2048
HD = 64
FF = 8192
SEQ_MAX = 512
GROUP = 1024
SEGS = 4
TOKENS = 4096
N_SHARD = 4


def draw_w_qkv(key, part):
    base = jax.random.normal(key, (3, D, D), jnp.float32) * D ** (-0.5)
    return jnp.clip(base, -1.0, 1.0).astype(jnp.bfloat16)


def levels(own_key, dims, pieces, low, high):
    loudness = 1.0
    for position, shards_of in pieces:
        draws = jax.random.uniform(jax.random.fold_in(jax.random.fold_in(own_key, 6), position), (shards_of,), jnp.float32, low / len(pieces), high / len(pieces))
        loudness = loudness * jnp.repeat(jnp.exp(draws), dims[position] // shards_of).reshape((-1,) + (1,) * (len(dims) - 1 - position))
    return loudness


def split_up(count, total, reach, skew):
    loads = [(1 << 20) // math.isqrt(rank ** skew) + 1 for rank in range(2, count + 1)]
    spare, holding = total - reach - (count - 1), [1] * (count - 1)
    while spare > 0:
        free = [i for i in range(count - 1) if holding[i] < reach]
        pool, budget = sum([loads[i] for i in free]), spare
        for i in free:
            extra = min(reach - holding[i], max(1, budget * loads[i] // pool), spare)
            holding[i] = holding[i] + extra
            spare = spare - extra
    return np.array([reach] + holding)


def uneven_parts(stream_key, number_of, total, limit, slope):
    if number_of == 2:
        one = jax.random.randint(stream_key, (), max(1, total - limit), min(limit, total - 1) + 1)
        return jnp.stack([one, total - one])
    lengths = jnp.asarray(split_up(number_of, total, limit, slope), jnp.int32)
    twos = (number_of - 1) // 2
    source_of, taker = lengths[1:1 + 2 * twos:2], lengths[2:2 + 2 * twos:2]
    room = jnp.minimum(source_of - 1, limit - taker)
    passed = jax.random.randint(jax.random.fold_in(stream_key, 1), (twos,), 0, 1 << 20) % (room + 1)
    lengths = lengths.at[1:1 + 2 * twos:2].set(source_of - passed).at[2:2 + 2 * twos:2].set(taker + passed)
    return lengths[jax.random.permutation(jax.random.fold_in(stream_key, 2), number_of)]


def bell_draw(own_key, shape, scale, most, split=(), kind=jnp.bfloat16):
    gain = levels(own_key, shape, split, -0.22, 0.18) if split else 1.0
    result = jax.random.normal(own_key, shape, jnp.float32) * scale * gain
    return jnp.minimum(jnp.maximum(result, -most), most).astype(kind)


def setup_inputs(seed: int = 0) -> dict:
    seeds = jax.random.split(jax.random.key(seed), 10)
    hidden_in = bell_draw(seeds[0], (TOKENS, D), 1.0, 6.0, ((0, 16),))
    gain_attn = jnp.clip(1.0 + 0.1 * jax.random.normal(seeds[1], (D,), jnp.float32), 0.5, 1.5).astype(jnp.bfloat16)
    w_qkv = draw_w_qkv(jax.random.fold_in(seeds[9], 71), 0)
    w_out = bell_draw(seeds[3], (D, D), (D // 16) ** -0.5, 0.5, ((0, 2), (1, 16)))
    gain_mlp = jnp.clip(1.0 + 0.1 * jax.random.normal(seeds[4], (D,), jnp.float32), 0.5, 1.5).astype(jnp.bfloat16)
    w_gate_up = bell_draw(seeds[5], (2, D, FF), D ** -0.5, 0.125, ((1, 16), (2, 2)))
    w_down = bell_draw(seeds[6], (FF, D), FF ** -0.5, 0.0625, ((0, 2), (1, 16)))
    segments = jax.vmap(lambda own: jnp.searchsorted(jnp.cumsum(uneven_parts(own, SEGS, GROUP, SEQ_MAX, 2)), jnp.arange(GROUP), side="right"))(jax.random.split(seeds[7], N_SHARD)).reshape((N_SHARD, GROUP)).astype(jnp.int32)
    cotangent = bell_draw(seeds[8], (TOKENS, D), 1.0, 6.0, ((0, 16),))
    return {"hidden_in": hidden_in, "gain_attn": gain_attn, "w_qkv": w_qkv, "w_out": w_out, "gain_mlp": gain_mlp, "w_gate_up": w_gate_up, "w_down": w_down, "segments": segments, "cotangent": cotangent}


EPSILON = 1e-05
ROPE_BASE = 130000.0
MASKED = -1e+30

def contract(form, left_in, right_in):
    return jnp.einsum(form, left_in.astype(jnp.float32), right_in.astype(jnp.float32))

def positions_of(seg_row):
    length_all = seg_row.shape[0]
    index_all = jnp.arange(length_all, dtype=jnp.int32)
    starts = jnp.concatenate([jnp.ones((1,), dtype=jnp.bool_), seg_row[1:] != seg_row[:-1]])
    first_index = lax.cummax(jnp.where(starts, index_all, jnp.zeros_like(index_all)), axis=0)
    return index_all - first_index

def rope_tables(positions, head_size):
    half_size = head_size // 2
    frequency = ROPE_BASE ** (-(jnp.arange(half_size, dtype=jnp.float32) * (2.0 / head_size)))
    angles = positions.astype(jnp.float32)[:, None] * frequency[None, :]
    return (jnp.cos(angles), jnp.sin(angles))

def rotate_heads(values_in, cosine_table, sine_table, head_size):
    rows_count = values_in.shape[0]
    shaped = values_in.reshape(rows_count, -1, head_size)
    half_size = head_size // 2
    first_half = shaped[..., :half_size]
    second_half = shaped[..., half_size:]
    cosine_rows = cosine_table[:, None, :]
    sine_rows = sine_table[:, None, :]
    turned = jnp.concatenate([first_half * cosine_rows - second_half * sine_rows, second_half * cosine_rows + first_half * sine_rows], -1)
    return turned.reshape(rows_count, -1)

def block_layout(array_in, block_rows):
    blocks_count = array_in.shape[0] // block_rows
    return array_in.reshape((blocks_count, block_rows) + array_in.shape[1:])

def with_previous(blocks, fill_value):
    earlier = jnp.concatenate([jnp.full_like(blocks[:1], fill_value), blocks[:-1]], 0)
    return jnp.concatenate([earlier, blocks], 1)

def block_masks(seg_row, block_rows):
    index_all = jnp.arange(seg_row.shape[0], dtype=jnp.int32)
    seg_query = block_layout(seg_row, block_rows)
    index_query = block_layout(index_all, block_rows)
    return (seg_query, index_query, with_previous(seg_query, -1), with_previous(index_query, 0))

def heads_view(array_in, head_size):
    return array_in.reshape(array_in.shape[0], -1, head_size)

def block_scores(query_blk, key_blk, seg_query_blk, index_query_blk, seg_key_blk, index_key_blk, head_size):
    allowed = (seg_key_blk[None, :] == seg_query_blk[:, None]) & (index_key_blk[None, :] <= index_query_blk[:, None])
    scores = contract('qhd,khd->hqk', query_blk, key_blk) * head_size ** (-0.5)
    return jnp.where(allowed[None], scores, MASKED)

def attention_forward(queries, keys_rot, value_vecs, seg_row, head_size):
    group_rows = queries.shape[0]
    block_rows = min(512, group_rows)
    query_blocks = block_layout(heads_view(queries, head_size), block_rows)
    key_blocks = with_previous(block_layout(heads_view(keys_rot, head_size), block_rows), 0)
    value_blocks = with_previous(block_layout(heads_view(value_vecs, head_size), block_rows), 0)
    seg_query, index_query, seg_keys, index_keys = block_masks(seg_row, block_rows)

    def one_block(block_items):
        query_blk, key_blk, value_blk, seg_qb, index_qb, seg_kb, index_kb = block_items
        scores = block_scores(query_blk, key_blk, seg_qb, index_qb, seg_kb, index_kb, head_size)
        row_max = lax.optimization_barrier(jnp.max(scores, -1, keepdims=True))
        log_total = row_max + jnp.log(lax.optimization_barrier(jnp.sum(jnp.exp(scores - row_max), -1, keepdims=True)))
        weights_low = jnp.exp(scores - log_total).astype(jnp.bfloat16)
        block_result = contract('hqk,khd->qhd', weights_low, value_blk)
        return (block_result.astype(jnp.bfloat16).reshape(block_rows, -1), log_total[..., 0])
    result_blocks, log_blocks = lax.map(one_block, (query_blocks, key_blocks, value_blocks, seg_query, index_query, seg_keys, index_keys))
    return (result_blocks.reshape(group_rows, -1), log_blocks)

def attention_backward(queries, keys_rot, value_vecs, attn, grad_attn, log_blocks, seg_row, head_size):
    group_rows = queries.shape[0]
    block_rows = min(512, group_rows)
    score_scale = head_size ** (-0.5)
    query_blocks = block_layout(heads_view(queries, head_size), block_rows)
    key_blocks = with_previous(block_layout(heads_view(keys_rot, head_size), block_rows), 0)
    value_blocks = with_previous(block_layout(heads_view(value_vecs, head_size), block_rows), 0)
    attn_blocks = block_layout(heads_view(attn, head_size), block_rows)
    grad_blocks = block_layout(heads_view(grad_attn, head_size), block_rows)
    seg_query, index_query, seg_keys, index_keys = block_masks(seg_row, block_rows)

    def one_block(block_items):
        query_blk, key_blk, value_blk, attn_blk, grad_blk, log_blk, seg_qb, index_qb, seg_kb, index_kb = block_items
        scores = block_scores(query_blk, key_blk, seg_qb, index_qb, seg_kb, index_kb, head_size)
        probs = jnp.exp(scores - log_blk[..., None])
        probs_low = probs.astype(jnp.bfloat16)
        grad_value_blk = contract('hqk,qhd->khd', probs_low, grad_blk)
        grad_probs = contract('qhd,khd->hqk', grad_blk, value_blk)
        diag = lax.optimization_barrier(jnp.sum(grad_blk.astype(jnp.float32) * attn_blk.astype(jnp.float32), -1)).T
        grad_scores = (probs * (grad_probs - diag[..., None])).astype(jnp.bfloat16)
        grad_query_blk = contract('hqk,khd->qhd', grad_scores, key_blk) * score_scale
        grad_key_blk = contract('hqk,qhd->khd', grad_scores, query_blk) * score_scale
        return (grad_query_blk, grad_key_blk, grad_value_blk)
    grad_query_b, grad_key_b, grad_value_b = lax.map(one_block, (query_blocks, key_blocks, value_blocks, attn_blocks, grad_blocks, log_blocks, seg_query, index_query, seg_keys, index_keys))

    def fold_pairs(pairs):
        earlier = pairs[:, :block_rows]
        current = pairs[:, block_rows:]
        shifted = jnp.concatenate([earlier[1:], jnp.zeros_like(earlier[:1])], 0)
        return (current + shifted).reshape(group_rows, -1).astype(jnp.bfloat16)
    return (grad_query_b.reshape(group_rows, -1).astype(jnp.bfloat16), fold_pairs(grad_key_b), fold_pairs(grad_value_b))

def group_pass(group_in, seg_row, group_cot, gain_attn, w_qkv, w_out, gain_mlp, w_gate_up, w_down):
    positions = positions_of(seg_row)
    cosine_table, sine_table = rope_tables(positions, HD)
    resid_in = group_in.astype(jnp.float32)
    scale_one = lax.rsqrt(lax.optimization_barrier(jnp.mean(resid_in * resid_in, -1, keepdims=True)) + EPSILON)
    gain_one = gain_attn.astype(jnp.float32)
    normed_one = (resid_in * scale_one * gain_one).astype(jnp.bfloat16)
    proj_query = jnp.dot(normed_one, w_qkv[0], preferred_element_type=jnp.float32)
    proj_key = jnp.dot(normed_one, w_qkv[1], preferred_element_type=jnp.float32)
    proj_value = jnp.dot(normed_one, w_qkv[2], preferred_element_type=jnp.float32)
    queries = rotate_heads(proj_query, cosine_table, sine_table, HD).astype(jnp.bfloat16)
    keys_rot = rotate_heads(proj_key, cosine_table, sine_table, HD).astype(jnp.bfloat16)
    value_vecs = proj_value.astype(jnp.bfloat16)
    attn, log_blocks = attention_forward(queries, keys_rot, value_vecs, seg_row, HD)
    resid_mid = resid_in + jnp.dot(attn, w_out, preferred_element_type=jnp.float32)
    scale_two = lax.rsqrt(lax.optimization_barrier(jnp.mean(resid_mid * resid_mid, -1, keepdims=True)) + EPSILON)
    gain_two = gain_mlp.astype(jnp.float32)
    normed_two = (resid_mid * scale_two * gain_two).astype(jnp.bfloat16)
    gate_proj = jnp.dot(normed_two, w_gate_up[0], preferred_element_type=jnp.float32)
    up_proj = jnp.dot(normed_two, w_gate_up[1], preferred_element_type=jnp.float32)
    sigmoid_gate = jax.nn.sigmoid(gate_proj)
    activated = (gate_proj * sigmoid_gate * up_proj).astype(jnp.bfloat16)
    block_out = (resid_mid + jnp.dot(activated, w_down, preferred_element_type=jnp.float32)).astype(jnp.bfloat16)
    grad_act = jnp.dot(group_cot, w_down.T, preferred_element_type=jnp.float32)
    grad_w_down = jnp.dot(activated.T, group_cot, preferred_element_type=jnp.float32)
    grad_gate = (grad_act * up_proj * sigmoid_gate * (1.0 + gate_proj * (1.0 - sigmoid_gate))).astype(jnp.bfloat16)
    grad_up = (grad_act * gate_proj * sigmoid_gate).astype(jnp.bfloat16)
    grad_w_gate_up = jnp.stack([jnp.dot(normed_two.T, grad_gate, preferred_element_type=jnp.float32), jnp.dot(normed_two.T, grad_up, preferred_element_type=jnp.float32)])
    grad_normed_two = jnp.dot(grad_gate, w_gate_up[0].T, preferred_element_type=jnp.float32) + jnp.dot(grad_up, w_gate_up[1].T, preferred_element_type=jnp.float32)
    grad_gain_mlp = lax.optimization_barrier(jnp.sum(grad_normed_two * resid_mid * scale_two, 0))
    scaled_two = grad_normed_two * gain_two
    grad_mid = group_cot.astype(jnp.float32) + scale_two * scaled_two - resid_mid * scale_two ** 3 * lax.optimization_barrier(jnp.mean(scaled_two * resid_mid, -1, keepdims=True))
    grad_mid_low = grad_mid.astype(jnp.bfloat16)
    grad_w_out = jnp.dot(attn.T, grad_mid_low, preferred_element_type=jnp.float32)
    grad_attn = jnp.dot(grad_mid_low, w_out.T, preferred_element_type=jnp.float32).astype(jnp.bfloat16)
    grad_queries, grad_keys, grad_values = attention_backward(queries, keys_rot, value_vecs, attn, grad_attn, log_blocks, seg_row, HD)
    pre_query = rotate_heads(grad_queries.astype(jnp.float32), cosine_table, -sine_table, HD).astype(jnp.bfloat16)
    pre_key = rotate_heads(grad_keys.astype(jnp.float32), cosine_table, -sine_table, HD).astype(jnp.bfloat16)
    grad_w_qkv = jnp.stack([jnp.dot(normed_one.T, pre_query, preferred_element_type=jnp.float32), jnp.dot(normed_one.T, pre_key, preferred_element_type=jnp.float32), jnp.dot(normed_one.T, grad_values, preferred_element_type=jnp.float32)])
    grad_normed_one = jnp.dot(pre_query, w_qkv[0].T, preferred_element_type=jnp.float32) + jnp.dot(pre_key, w_qkv[1].T, preferred_element_type=jnp.float32) + jnp.dot(grad_values, w_qkv[2].T, preferred_element_type=jnp.float32)
    grad_gain_attn = lax.optimization_barrier(jnp.sum(grad_normed_one * resid_in * scale_one, 0))
    scaled_one = grad_normed_one * gain_one
    grad_input = grad_mid + scale_one * scaled_one - resid_in * scale_one ** 3 * lax.optimization_barrier(jnp.mean(scaled_one * resid_in, -1, keepdims=True))
    return (block_out, grad_input, (grad_gain_attn, grad_w_qkv, grad_w_out, grad_gain_mlp, grad_w_gate_up, grad_w_down))

def reference(hidden_in, gain_attn, w_qkv, w_out, gain_mlp, w_gate_up, w_down, segments, cotangent):
    groups_count = segments.shape[0]
    group_rows = segments.shape[1]
    width = hidden_in.shape[1]
    inputs_grouped = hidden_in.reshape(groups_count, group_rows, width)
    cot_grouped = cotangent.reshape(groups_count, group_rows, width)
    zero_grads = (jnp.zeros(gain_attn.shape, jnp.float32), jnp.zeros(w_qkv.shape, jnp.float32), jnp.zeros(w_out.shape, jnp.float32), jnp.zeros(gain_mlp.shape, jnp.float32), jnp.zeros(w_gate_up.shape, jnp.float32), jnp.zeros(w_down.shape, jnp.float32))

    def one_group(totals, group_items):
        group_in, seg_row, group_cot = group_items
        block_out, grad_input, grads = group_pass(group_in, seg_row, group_cot, gain_attn, w_qkv, w_out, gain_mlp, w_gate_up, w_down)
        return (jax.tree.map(lambda left_in, right_in: left_in + right_in, totals, grads), (block_out, grad_input))
    totals, (outs_grouped, grads_grouped) = lax.scan(one_group, zero_grads, (inputs_grouped, segments, cot_grouped))
    return (outs_grouped.reshape(-1, width), grads_grouped.reshape(-1, width), totals[0], totals[1], totals[2], totals[3], totals[4], totals[5])
```

```python
import functools
import jax
import jax.numpy as jnp
from jax import lax
from jax.experimental import pallas as pl
from jax.experimental.pallas import tpu as pltpu
from jax.sharding import PartitionSpec as P

HD = 64
SEQ_MAX = 512
EPSILON = 1e-05
ROPE_BASE = 130000.0
MASKED = -1e30
HALF = HD // 2


def dot(left_in, right_in, left_dim, right_dim):
    return lax.dot_general(
        left_in, right_in, (((left_dim,), (right_dim,)), ((), ())), preferred_element_type=jnp.float32
    )


def half_swap(values_in):
    width = values_in.shape[1]
    if width == HD:
        return jnp.concatenate([values_in[:, HALF:], values_in[:, :HALF]], 1)
    lanes = lax.broadcasted_iota(jnp.int32, values_in.shape, 1)
    return jnp.where(
        lanes % HD < HALF,
        pltpu.roll(values_in, width - HALF, 1),
        pltpu.roll(values_in, HALF, 1),
    )


def chunk_start(own_chunk, chunk, chunks, rows):
    return pl.multiple_of(lax.rem(own_chunk - chunk + chunks, chunks) * rows, rows)


def group_start(step, columns, width):
    if columns == width:
        return 0
    return pl.multiple_of(step // (width // HD) * width, width)


def block_allowed(start_ref, index_ref, key_index_ref, q_at, k_at, rows):
    first = start_ref[pl.ds(q_at, rows), :]
    last = index_ref[pl.ds(q_at, rows), :]
    keys = jnp.concatenate([key_index_ref[:, pl.ds(at, rows)] for at in k_at], 1)
    return (keys >= first) & (keys <= last)


def attend_kernel(
    chunks, own_ref, proj_ref, cos_ref, sin_ref, start_ref, index_ref, key_index_ref,
    qkv_ref, attn_ref, log_ref,
):
    tokens, columns = attn_ref.shape
    rows = tokens // chunks
    width = min(128, columns)
    own = own_ref[0]

    def turn(step, carry):
        at = pl.multiple_of(step * rows, rows)
        cosine = cos_ref[pl.ds(at, rows), :]
        sine = sin_ref[pl.ds(at, rows), :]
        for first in range(0, 2 * columns, width):
            part = proj_ref[pl.ds(at, rows), first : first + width]
            scale = HD**-0.5 if first < columns else 1.0
            turned = (part * cosine + half_swap(part) * sine).astype(jnp.bfloat16)
            qkv_ref[first // columns, pl.ds(at, rows), first % columns : first % columns + width] = (
                turned * jnp.bfloat16(scale)
            )
        qkv_ref[2, pl.ds(at, rows), :] = proj_ref[pl.ds(at, rows), 2 * columns :].astype(
            jnp.bfloat16
        )
        return carry

    lax.fori_loop(0, chunks, turn, 0)
    lanes = lax.broadcasted_iota(jnp.int32, (rows, width), 1)
    reach = -(-(SEQ_MAX - 1) // rows)
    for chunk in range(chunks):
        q_at = chunk_start(own, chunk, chunks, rows)
        k_at = [chunk_start(own, b, chunks, rows) for b in range(max(0, chunk - reach), chunk + 1)]

        def head(step, carry, q_at=q_at, k_at=k_at):
            at = group_start(step, columns, width)
            mine = lanes // HD == step % (width // HD)
            query = jnp.where(mine, qkv_ref[0, pl.ds(q_at, rows), pl.ds(at, width)], 0)
            keys = jnp.concatenate(
                [qkv_ref[1, pl.ds(b, rows), pl.ds(at, width)] for b in k_at], 0
            )
            values = jnp.concatenate(
                [qkv_ref[2, pl.ds(b, rows), pl.ds(at, width)] for b in k_at], 0
            )
            allowed = block_allowed(start_ref, index_ref, key_index_ref, q_at, k_at, rows)
            scores = jnp.where(allowed, dot(query, keys, 1, 1), MASKED)
            row_max = jnp.max(scores, -1, keepdims=True)
            powers = jnp.exp(scores - row_max)
            total = jnp.sum(powers, -1, keepdims=True)
            weights = (powers * (1.0 / total)).astype(jnp.bfloat16)
            result = dot(weights, values, 1, 0).astype(jnp.bfloat16)
            log_total = jnp.broadcast_to(row_max + jnp.log(total), result.shape)
            where = (pl.ds(q_at, rows), pl.ds(at, width))
            attn_ref[where] = jnp.where(mine, result, attn_ref[where])
            log_ref[where] = jnp.where(mine, log_total, log_ref[where])
            return carry

        lax.fori_loop(0, columns // HD, head, 0)


def attend_back_kernel(
    chunks, own_ref, qkv_ref, attn_ref, grad_ref, log_ref, cos_ref, sin_ref, start_ref, index_ref,
    key_index_ref, out_ref, dq_ref, dk_ref, dv_ref,
):
    tokens, columns = attn_ref.shape
    rows = tokens // chunks
    width = min(128, columns)
    own = own_ref[0]
    dq_ref[...] = jnp.zeros_like(dq_ref)
    dk_ref[...] = jnp.zeros_like(dk_ref)
    dv_ref[...] = jnp.zeros_like(dv_ref)
    lanes = lax.broadcasted_iota(jnp.int32, (rows, width), 1)
    reach = -(-(SEQ_MAX - 1) // rows)
    for chunk in range(chunks):
        q_at = chunk_start(own, chunk, chunks, rows)
        k_at = [chunk_start(own, b, chunks, rows) for b in range(max(0, chunk - reach), chunk + 1)]

        def head(step, carry, q_at=q_at, k_at=k_at):
            at = group_start(step, columns, width)
            mine = lanes // HD == step % (width // HD)
            where = (pl.ds(q_at, rows), pl.ds(at, width))
            query = jnp.where(mine, qkv_ref[(0,) + where], 0)
            keys = jnp.concatenate(
                [qkv_ref[1, pl.ds(b, rows), pl.ds(at, width)] for b in k_at], 0
            )
            values = jnp.concatenate(
                [qkv_ref[2, pl.ds(b, rows), pl.ds(at, width)] for b in k_at], 0
            )
            grad = jnp.where(mine, grad_ref[where], 0)
            diag = jnp.sum(
                grad.astype(jnp.float32) * attn_ref[where].astype(jnp.float32), -1, keepdims=True
            )
            log_total = jnp.max(jnp.where(mine, log_ref[where], MASKED), -1, keepdims=True)
            allowed = block_allowed(start_ref, index_ref, key_index_ref, q_at, k_at, rows)
            scores = dot(query, keys, 1, 1)
            probs = jnp.where(allowed, jnp.exp(scores - log_total), 0.0)
            grad_probs = dot(grad, values, 1, 1)
            grad_scores = (probs * (grad_probs - diag)).astype(jnp.bfloat16)
            dq_ref[where] += jnp.where(mine, dot(grad_scores, keys, 1, 0), 0.0)
            grad_keys = dot(grad_scores, query, 0, 0)
            grad_values = dot(probs.astype(jnp.bfloat16), grad, 0, 0)
            for place, b in enumerate(k_at):
                span = (pl.ds(b, rows), pl.ds(at, width))
                dk_ref[span] += grad_keys[place * rows : (place + 1) * rows]
                dv_ref[span] += grad_values[place * rows : (place + 1) * rows]
            return carry

        lax.fori_loop(0, columns // HD, head, 0)

    def turn(step, carry):
        at = pl.multiple_of(step * rows, rows)
        cosine = cos_ref[pl.ds(at, rows), :]
        sine = sin_ref[pl.ds(at, rows), :]
        for first in range(0, columns, width):
            part = dq_ref[pl.ds(at, rows), first : first + width] * (HD**-0.5)
            out_ref[pl.ds(at, rows), first : first + width] = (
                part * cosine - half_swap(part) * sine
            ).astype(jnp.bfloat16)
            part = dk_ref[pl.ds(at, rows), first : first + width]
            out_ref[pl.ds(at, rows), columns + first : columns + first + width] = (
                part * cosine - half_swap(part) * sine
            ).astype(jnp.bfloat16)
        out_ref[pl.ds(at, rows), 2 * columns :] = dv_ref[pl.ds(at, rows), :].astype(jnp.bfloat16)
        return carry

    lax.fori_loop(0, chunks, turn, 0)


def in_vmem(count):
    return [pl.BlockSpec(memory_space=pltpu.SMEM)] + [pl.BlockSpec(memory_space=pltpu.VMEM)] * count


def attend(chunks, own, projected, tables):
    tokens = projected.shape[0]
    columns = projected.shape[1] // 3
    return pl.pallas_call(
        functools.partial(attend_kernel, chunks),
        out_shape=(
            jax.ShapeDtypeStruct((3, tokens, columns), jnp.bfloat16),
            jax.ShapeDtypeStruct((tokens, columns), jnp.bfloat16),
            jax.ShapeDtypeStruct((tokens, columns), jnp.float32),
        ),
        in_specs=in_vmem(6),
        out_specs=tuple([pl.BlockSpec(memory_space=pltpu.VMEM)] * 3),
        compiler_params=pltpu.CompilerParams(vmem_limit_bytes=40 << 20),
        cost_estimate=pl.CostEstimate(
            flops=4 * tokens * tokens * columns // 2,
            bytes_accessed=24 * tokens * columns,
            transcendentals=tokens * tokens * columns // HD // 2,
        ),
        name="attend",
    )(own, projected, *tables)


def attend_back(chunks, own, qkv, attn, grad_attn, logs, tables):
    tokens, columns = attn.shape
    return pl.pallas_call(
        functools.partial(attend_back_kernel, chunks),
        out_shape=jax.ShapeDtypeStruct((tokens, 3 * columns), jnp.bfloat16),
        in_specs=in_vmem(9),
        out_specs=pl.BlockSpec(memory_space=pltpu.VMEM),
        scratch_shapes=[pltpu.VMEM((tokens, columns), jnp.float32)] * 3,
        compiler_params=pltpu.CompilerParams(vmem_limit_bytes=40 << 20),
        cost_estimate=pl.CostEstimate(
            flops=10 * tokens * tokens * columns // 2,
            bytes_accessed=24 * tokens * columns,
            transcendentals=tokens * tokens * columns // HD // 2,
        ),
        name="attend_back",
    )(own, qkv, attn, grad_attn, logs, *tables)


def bits_of(count):
    return [1 << b for b in range(count.bit_length() - 1)]


def flip(array_in, axis, bit):
    size = lax.axis_size(axis)
    return lax.ppermute(array_in, axis, [(i, i ^ bit) for i in range(size)])


def shift(array_in, axis, step):
    size = lax.axis_size(axis)
    return lax.ppermute(array_in, axis, [(i, (i + step) % size) for i in range(size)])


class Turn:
    def __init__(self, event=None):
        self.event = event

    def shift(self, array_in, axis, step):
        if self.event is not None:
            array_in = lax.optimization_barrier((array_in, self.event))[0]
        self.event = shift(array_in, axis, step)
        return self.event


class Free:
    def shift(self, array_in, axis, step):
        return shift(array_in, axis, step)


def cut_blocks(array_in, dim, indices, rows):
    return [lax.dynamic_slice_in_dim(array_in, i * rows, rows, dim) for i in indices]


def by_sender(pieces, axis):
    size = len(pieces)
    own = lax.axis_index(axis)
    line = jnp.stack(pieces)
    return [lax.dynamic_index_in_dim(line, (own - i) % size, 0, False) for i in range(size)]


def xor_columns(array_in, axis):
    size = lax.axis_size(axis)
    own = lax.axis_index(axis)
    wide = array_in.shape[1] // size
    return jnp.concatenate(cut_blocks(array_in, 1, [r ^ own for r in range(size)], wide), 1)


def tp_pair():
    return lax.axis_size("tp") == 2


def tp_gather(own):
    if tp_pair():
        return [own, flip(own, "tp", 1)]
    return [lax.all_gather(own, "tp", axis=0, tiled=True)]


def tp_reduce(terms):
    if tp_pair():
        half = terms.shape[0] // 2
        low = terms.astype(jnp.bfloat16)
        return terms[:half] + flip(low[half:], "tp", 1).astype(jnp.float32)
    return lax.psum_scatter(
        terms.astype(jnp.bfloat16), "tp", scatter_dimension=0, tiled=True
    ).astype(jnp.float32)


def tp_rows(rows_in):
    size = lax.axis_size("tp")
    rows = rows_in.shape[0] // size
    own = lax.axis_index("tp")
    mine = lax.dynamic_slice_in_dim(rows_in, own * rows, rows)
    if tp_pair():
        return mine, [mine, lax.dynamic_slice_in_dim(rows_in, (1 - own) * rows, rows)]
    return mine, [rows_in]


def gather_tokens(own, turn, chunk=None):
    parts = tp_gather(own) if chunk is None else list(chunk)
    passed = own
    for _ in range(lax.axis_size("ctx") - 1):
        passed = turn.shift(passed, "ctx", 1)
        parts += tp_gather(passed)
    return jnp.concatenate(parts, 0)


def reduce_tokens(terms_of, turn):
    size = lax.axis_size("ctx")
    total = None
    for j in [(1 + m) % size for m in range(size)]:
        mine = tp_reduce(terms_of(j))
        if total is not None:
            mine = mine + turn.shift(total.astype(jnp.bfloat16), "ctx", 1).astype(jnp.float32)
        total = mine
    return total


def spread(local_rows, turn):
    size = lax.axis_size("ctx")
    own = lax.axis_index("ctx")
    columns = local_rows.shape[1] // size
    cuts = cut_blocks(local_rows, 1, [(own + m) % size for m in range(size)], columns)
    pieces = [cuts[0]] + [turn.shift(cuts[m], "ctx", m) for m in range(1, size)]
    return jnp.concatenate(by_sender(pieces, "ctx"), 0)


def gather_shards(own):
    placed = {0: own}
    for bit in reversed(bits_of(lax.axis_size("shard"))):
        placed.update({r | bit: flip(block, "shard", bit) for r, block in list(placed.items())})
    return jnp.concatenate([placed[r] for r in range(len(placed))], 0)


def reduce_shards(terms_of):
    def reduced(r, level):
        if level == 0:
            return terms_of(r)
        bit = 1 << (level - 1)
        theirs = reduced(r | bit, level - 1).astype(jnp.bfloat16)
        return reduced(r, level - 1) + flip(theirs, "shard", bit).astype(jnp.float32)

    return reduced(0, len(bits_of(lax.axis_size("shard"))))


def own_columns(rows_of_ctx, turn):
    size = lax.axis_size("ctx")
    own = lax.axis_index("ctx")
    rows = rows_of_ctx.shape[0] // size
    cuts = cut_blocks(rows_of_ctx, 0, [(own + m) % size for m in range(size)], rows)
    pieces = [cuts[0]] + [turn.shift(cuts[m], "ctx", m) for m in range(1, size)]
    return by_sender(pieces, "ctx")


def norm_backward(grad_scaled, resid, scale):
    return scale * grad_scaled - resid * scale**3 * jnp.mean(
        grad_scaled * resid, -1, keepdims=True
    )


def token_tables(seg_row, chunk_rows, columns):
    ctx_size, tp_size = lax.axis_size("ctx"), lax.axis_size("tp")
    length = seg_row.shape[0]
    index_all = jnp.arange(length, dtype=jnp.int32)
    starts = jnp.concatenate([jnp.ones((1,), dtype=jnp.bool_), seg_row[1:] != seg_row[:-1]])
    first_all = lax.cummax(jnp.where(starts, index_all, jnp.zeros_like(index_all)), axis=0)
    chunk = (lax.axis_index("ctx") - jnp.arange(ctx_size)) % ctx_size
    sub = jnp.arange(tp_size)
    if tp_pair():
        sub = sub ^ lax.axis_index("tp")
    blocks = (chunk[:, None] * tp_size + sub[None, :]).reshape(-1)
    rows = chunk_rows // tp_size
    index = (blocks[:, None] * rows + jnp.arange(rows)[None, :]).reshape(-1).astype(jnp.int32)
    first = first_all.reshape(-1, rows)[blocks].reshape(-1)
    frequency = ROPE_BASE ** (-(jnp.arange(HALF, dtype=jnp.float32) * (2.0 / HD)))
    angles = (index - first).astype(jnp.float32)[:, None] * frequency[None, :]
    cosine, sine = jnp.cos(angles), jnp.sin(angles)
    heads = min(128, columns) // HD
    return (
        jnp.concatenate([cosine, cosine] * heads, 1),
        jnp.concatenate([-sine, sine] * heads, 1),
        first[:, None],
        index[:, None],
        index[None, :],
    )


def on_device(hidden_in, gain_attn, w_qkv, w_out, gain_mlp, w_gate_up, w_down, segments, cotangent):
    ctx_size = lax.axis_size("ctx")
    shard_size = lax.axis_size("shard")
    chunk_rows, width = hidden_in.shape
    columns = w_out.shape[0] // ctx_size
    own_ctx = lax.axis_index("ctx").astype(jnp.int32)[None]
    tables = token_tables(segments[0], chunk_rows, columns)
    gain_one = gain_attn.astype(jnp.float32)[:, None]
    gain_two = gain_mlp.astype(jnp.float32)[:, None]

    def scaled(weights, gain):
        return (weights.astype(jnp.float32) * gain).astype(jnp.bfloat16)

    def normed(rows_in):
        wide = rows_in.astype(jnp.float32)
        scale = lax.rsqrt(jnp.mean(wide * wide, -1, keepdims=True) + EPSILON)
        return scale, (wide * scale).astype(jnp.bfloat16)

    hidden_own, hidden_chunk = tp_rows(xor_columns(hidden_in, "shard"))
    cot_own, cot_chunk = tp_rows(xor_columns(cotangent, "shard"))
    resid_in = hidden_own.astype(jnp.float32)
    scale_one, normed_own = normed(hidden_own)

    kinds = w_qkv.shape[0]
    free = Free()
    first_turn = Turn()
    qkv_full = jnp.concatenate(
        [gather_shards(spread(scaled(w_qkv[k], gain_one), free)) for k in range(kinds)], 1
    )
    normed_one = gather_tokens(normed_own, first_turn, [normed(part)[1] for part in hidden_chunk])
    bulk = Turn(first_turn.event)
    out_full = gather_shards(spread(w_out.T, bulk))
    gate_full = gather_shards(spread(scaled(w_gate_up[0], gain_two), bulk))
    cot_all = gather_tokens(cot_own, bulk, cot_chunk)
    up_full = gather_shards(spread(scaled(w_gate_up[1], gain_two), bulk))
    down_full = gather_shards(spread(w_down.T, bulk))
    gate_up_full = jnp.concatenate([gate_full, up_full], 1)

    def chunk_of(array_in, j):
        return array_in[j * chunk_rows : (j + 1) * chunk_rows]

    def rows_of_shard(array_in, r):
        rows = width // shard_size
        return array_in[:, r * rows : (r + 1) * rows]

    def own_gradient(tokens_wide, tokens_grad, turn):
        whole = reduce_shards(lambda r: dot(rows_of_shard(tokens_wide, r), tokens_grad, 0, 0))
        return own_columns(whole.astype(jnp.bfloat16), turn)

    projected = dot(normed_one, qkv_full, 1, 0)
    qkv, attn, logs = attend(ctx_size, own_ctx, projected, tables)
    resid_mid = resid_in + reduce_tokens(lambda j: dot(chunk_of(attn, j), out_full, 1, 1), free)
    scale_two, normed_two_own = normed(resid_mid)
    normed_two = gather_tokens(normed_two_own, free)
    gate_up = dot(normed_two, gate_up_full, 1, 0)
    gate_proj, up_proj = jnp.split(gate_up, 2, axis=1)
    sigmoid_gate = jax.nn.sigmoid(gate_proj)
    activated = (gate_proj * sigmoid_gate * up_proj).astype(jnp.bfloat16)

    grad_act = dot(cot_all, down_full, 1, 0)
    grad_gate = grad_act * up_proj * sigmoid_gate * (1.0 + gate_proj * (1.0 - sigmoid_gate))
    grad_up = grad_act * gate_proj * sigmoid_gate
    grad_pair = jnp.concatenate([grad_gate, grad_up], 1).astype(jnp.bfloat16)
    scaled_two = reduce_tokens(lambda j: dot(chunk_of(grad_pair, j), gate_up_full, 1, 1), free)
    grad_mid = cot_own.astype(jnp.float32) + norm_backward(scaled_two, resid_mid, scale_two)
    grad_mid_all = gather_tokens(grad_mid.astype(jnp.bfloat16), free)
    grad_attn = dot(grad_mid_all, out_full, 1, 0).astype(jnp.bfloat16)

    late = Turn(scaled_two)
    mlp_sum = reduce_tokens(lambda j: dot(chunk_of(activated, j), down_full, 1, 1), late)
    block_own = (resid_mid + mlp_sum).astype(jnp.bfloat16)

    def to_owner(own):
        both = jnp.concatenate(tp_gather(own), 0)
        if tp_pair():
            tp_own = lax.axis_index("tp")
            both = jnp.concatenate(
                cut_blocks(both, 0, [tp_own, 1 - tp_own], own.shape[0]), 0
            )
        return xor_columns(both, "shard")

    block_out = to_owner(block_own)
    down_parts = own_gradient(cot_all, activated, late)
    gate_up_parts = own_gradient(normed_two, grad_pair, late)
    out_parts = own_gradient(grad_mid_all, attn, late)

    grad_proj = attend_back(ctx_size, own_ctx, qkv, attn, grad_attn, logs, tables)
    scaled_one = reduce_tokens(lambda j: dot(chunk_of(grad_proj, j), qkv_full, 1, 1), free)
    grad_own = grad_mid + norm_backward(scaled_one, resid_in, scale_one)
    grad_input = to_owner(grad_own.astype(jnp.bfloat16)).astype(jnp.float32)
    qkv_parts = own_gradient(normed_one, grad_proj, free)

    def unpack_in(parts, gain, weights):
        each = parts[0].shape[1] // weights.shape[0]
        raw = jnp.stack(
            [
                jnp.concatenate([part[:, k * each : (k + 1) * each] for part in parts], 1)
                for k in range(weights.shape[0])
            ]
        ).astype(jnp.float32)
        return raw * gain[None], jnp.sum(raw * weights.astype(jnp.float32), (0, 2))

    def unpack_out(parts):
        return jnp.concatenate([part.T for part in parts], 0).astype(jnp.float32)

    grad_w_gate_up, gain_two_term = unpack_in(gate_up_parts, gain_two, w_gate_up)
    grad_w_qkv, gain_one_term = unpack_in(qkv_parts, gain_one, w_qkv)
    gain_terms = jnp.stack([gain_one_term, gain_two_term])
    gain_grads = gain_terms + flip(gain_terms, "tp", 1) if tp_pair() else lax.psum(gain_terms, "tp")
    return (
        block_out,
        grad_input,
        gain_grads[0],
        grad_w_qkv,
        unpack_out(out_parts),
        gain_grads[1],
        grad_w_gate_up,
        unpack_out(down_parts),
    )


def solution(mesh):
    placed = (
        P(("shard", "ctx"), None),
        P(("shard", "ctx")),
        P(None, ("shard", "ctx"), "tp"),
        P("tp", ("shard", "ctx")),
        P(("shard", "ctx")),
        P(None, ("shard", "ctx"), "tp"),
        P("tp", ("shard", "ctx")),
        P("shard", None),
        P(("shard", "ctx"), None),
    )
    return jax.shard_map(
        on_device,
        mesh=mesh,
        in_specs=placed,
        out_specs=(
            P(("shard", "ctx"), None),
            P(("shard", "ctx"), None),
            P(("shard", "ctx")),
            P(None, ("shard", "ctx"), "tp"),
            P("tp", ("shard", "ctx")),
            P(("shard", "ctx")),
            P(None, ("shard", "ctx"), "tp"),
            P("tp", ("shard", "ctx")),
        ),
        check_vma=False,
    )
```
